512 devices in a mesh: replica: 8 (over y_lo, core), shard: 64 (over z, y_hi, x).
Axes of the slice: x: 4, y: 8 (y_hi: 2, y_lo: 4; y = y_hi * 4 + y_lo), z: 8, core: 2. Of those that a mesh axis runs over, the one named last changes fastest.
Arguments:
- gradients: bfloat16 [8, 2, 64, 1024, 256], P('replica', None, None, 'shard'), may hold values from -36 to 36
- momentum: float32 [8, 64, 1024, 256], P('replica', None, 'shard'), may hold values from -3 to 3
- params: float32 [64, 1024, 256], P(None, ('shard', 'replica')), may hold values from -6 to 6
- outer_moment: float32 [64, 1024, 256], P(None, ('shard', 'replica')), may hold values from -2 to 2
- shadow: float32 [64, 1024, 256], P(None, ('shard', 'replica')), may hold values from -6 to 6
Outputs:
- new_params: float32 [64, 1024, 256], P(None, ('shard', 'replica'))
- new_outer_moment: float32 [64, 1024, 256], P(None, ('shard', 'replica'))
- new_shadow: float32 [64, 1024, 256], P(None, ('shard', 'replica'))
- new_momentum: float32 [8, 64, 1024, 256], P('replica', None, 'shard')
The draws below stay inside these ranges and needn't reach their ends.
All inputs are finite; a program needn't handle non-finite values.
Results may differ from the reference program's by a relative error of at most 0.0085.
Values may be sent and summed in bfloat16 or wider, within the bound.
A program may use at most 64 MiB of HBM per device.

```python
import math
import jax
import jax.numpy as jnp
from jax import lax

D = 1024
FF = 256
INNER = 2
NS_ITERS = 5
MATS = 64
N_REPLICA = 8


def draw_gradients(key, part):
    shape = (N_REPLICA, INNER, MATS, D, FF)
    key_base, key_rows, key_cols = jax.random.split(key, 3)
    row_scale = jnp.exp(jax.random.uniform(key_rows, (N_REPLICA, INNER, MATS, D, 1), jnp.float32, math.log(0.3), math.log(3.0)))
    col_scale = jnp.exp(jax.random.uniform(key_cols, (N_REPLICA, INNER, MATS, 1, FF), jnp.float32, math.log(0.3), math.log(3.0)))
    base = jnp.clip(jax.random.normal(key_base, shape, jnp.float32), -4.0, 4.0)
    return (base * row_scale * col_scale).astype(jnp.bfloat16)


def block_scale(key, dims, pieces, least, top_value):
    def one(dim, parts):
        draws = jax.random.uniform(jax.random.fold_in(jax.random.fold_in(key, 6), dim), (parts,), jnp.float32, least / len(pieces), top_value / len(pieces))
        return jnp.repeat(jnp.exp(draws), dims[dim] // parts).reshape((-1,) + (1,) * (len(dims) - dim - 1))

    gain = one(*pieces[0])
    for cut in pieces[1:]:
        gain = gain * one(*cut)
    return gain


def bell_draw(own_key, shape, width, limit, pieces=(), kind=jnp.bfloat16):
    level = block_scale(own_key, shape, pieces, -0.22, 0.18) if pieces else 1.0
    array = jax.random.normal(own_key, shape, jnp.float32) * width * level
    return jnp.minimum(jnp.maximum(array, -limit), limit).astype(kind)


def setup_inputs(seed: int = 0) -> dict:
    key_list = jax.random.split(jax.random.key(seed), 6)
    gradients = draw_gradients(jax.random.fold_in(key_list[5], 71), 0)
    momentum = bell_draw(key_list[1], (N_REPLICA, MATS, D, FF), 0.5, 3.0, ((0, 8), (2, 64)), jnp.float32)
    params = bell_draw(key_list[2], (MATS, D, FF), 1.0, 6.0, ((1, 512),), jnp.float32)
    outer_moment = bell_draw(key_list[3], (MATS, D, FF), 0.3, 2.0, ((1, 512),), jnp.float32)
    shadow = bell_draw(key_list[4], (MATS, D, FF), 1.0, 6.0, ((1, 512),), jnp.float32)
    return {"gradients": gradients, "momentum": momentum, "params": params, "outer_moment": outer_moment, "shadow": shadow}


quintic_a = 3.4445
quintic_b = -4.775
quintic_c = 2.0315
inner_beta = 0.95
outer_mu = 0.9
outer_rate = 0.7
shadow_decay = 0.9

def orthogonalize(update):
    squares = jnp.sum(jnp.square(update.astype(jnp.float32)))
    current = (update.astype(jnp.float32) / (jnp.sqrt(squares) + 1e-07)).astype(jnp.bfloat16)
    for repeat in range(NS_ITERS):
        gram_block = jnp.dot(current.T, current, preferred_element_type=jnp.float32).astype(jnp.bfloat16)
        square = jnp.dot(gram_block, gram_block, preferred_element_type=jnp.float32)
        polynomial = (quintic_b * gram_block.astype(jnp.float32) + quintic_c * square).astype(jnp.bfloat16)
        product = jnp.dot(current, polynomial, preferred_element_type=jnp.float32)
        current = (quintic_a * current.astype(jnp.float32) + product).astype(jnp.bfloat16)
    return current

def reference(gradients, momentum, params, outer_moment, shadow):
    scale_step = 0.2 * math.sqrt(D)
    deltas = jnp.zeros(params.shape, jnp.float32)
    moments = []
    for replica in range(N_REPLICA):
        moment_now = momentum[replica]
        total = jnp.zeros(params.shape, jnp.float32)
        for position in range(INNER):
            grad_now = gradients[replica, position].astype(jnp.float32)
            moment_now = inner_beta * moment_now + grad_now
            update = (grad_now + inner_beta * moment_now).astype(jnp.bfloat16)
            orthos = lax.map(orthogonalize, update)
            total = total + scale_step * orthos.astype(jnp.float32)
        deltas = deltas + total
        moments.append(moment_now)
    outer_delta = deltas / N_REPLICA
    new_outer = outer_mu * outer_moment + outer_delta
    new_params = params - outer_rate * (outer_delta + outer_mu * new_outer)
    new_shadow = shadow_decay * shadow + (1.0 - shadow_decay) * new_params
    return (new_params, new_outer, new_shadow, jnp.stack(moments))
```

```python
import functools
import math

import jax
import jax.numpy as jnp
from jax import lax
from jax.experimental import pallas as pl
from jax.experimental.pallas import tpu as pltpu
from jax.sharding import PartitionSpec as P

D = 1024
FF = 256
INNER = 2
NS_ITERS = 5
MATS = 64
ROWS = 16

quintic_a = 3.4445
quintic_b = -4.775
quintic_c = 2.0315
inner_beta = 0.95
outer_mu = 0.9
outer_rate = 0.7
shadow_decay = 0.9
scale_step = 0.2 * math.sqrt(D)

MESH = pl.DeviceIdType.MESH
f32, bf16 = jnp.float32, jnp.bfloat16
NT = (((1,), (1,)), ((), ()))
NN = (((1,), (0,)), ((), ()))


def place():
    replica, shard = lax.axis_index("replica"), lax.axis_index("shard")
    core, y_lo = replica % 2, replica // 2
    x, y_hi, z = shard % 4, (shard // 4) % 2, shard // 8
    return x, y_hi * 4 + y_lo, z, core


def device(x, y, z, core):
    return {"replica": (y % 4) * 2 + core, "shard": z * 8 + (y // 4) * 4 + x}


def spread(j):
    j = (3 * j) % 8
    half = (j + 1) // 2
    return (8 + half * (2 * (j % 2) - 1)) % 8


def offsets(i):
    outer, inner = i // 8, i % 8
    return spread((5 * inner + outer) % 8), spread(inner)


def dot(a, b, dims):
    return lax.dot_general(a, b, dims, preferred_element_type=f32)


def newton_schulz(update):
    wide = update.astype(f32)
    squares = jnp.sum(wide * wide)
    current = (wide / (jnp.sqrt(squares) + 1e-07)).astype(bf16).T
    for _ in range(NS_ITERS):
        gram = dot(current, current, NT).astype(bf16)
        square = dot(gram, gram, NN)
        poly = (quintic_b * gram.astype(f32) + quintic_c * square).astype(bf16)
        current = (quintic_a * current.astype(f32) + dot(poly, current, NN)).astype(bf16)
    return current


def wait_bytes(ref, sem):
    pltpu.make_async_copy(ref, ref, sem).wait()


def exchange_kernel(u0, u1, out, own, first, delta, parts, reduced, gathered,
                    send_a, recv_a, send_b, recv_b, send_c, recv_c):
    x, y, z, core = place()
    mine = z * 8 + y
    shard = z * 8 + (y // 4) * 4 + x
    x_of = lambda y_m: (y % 4 + y_m) % 4
    self_a = x_of(y) == x
    self_c = core == z // 4

    barrier = pltpu.get_barrier_semaphore()

    def greet(x, y, z, core):
        pl.semaphore_signal(barrier, 1, device_id=device(x, y, z, core), device_id_type=MESH)

    def greet_a(i, _):
        sx, syh, sz = i % 4, (i // 4) % 2, i // 8
        sy = syh * 4 + (x + 8 - y) % 4

        @pl.when(jnp.logical_not((sx == x) & (sy == y) & (sz == z)))
        def _():
            greet(sx, sy, sz, core)

        return 0

    def greet_c(i, _):
        sy, sz, sc = i % 8, i // 8, z // 4

        @pl.when(jnp.logical_not((sy == y) & (sz == z) & (sc == core)))
        def _():
            greet(x, sy, sz, sc)

        return 0

    lax.fori_loop(0, 64, greet_a, 0)
    for j in range(1, 8):
        greet((x + j // 2) % 4, y, z, (core + j) % 2)
    lax.fori_loop(0, 64, greet_c, 0)
    pl.semaphore_wait(
        barrier, 64 + 7 + 64 - self_a.astype(jnp.int32) - self_c.astype(jnp.int32)
    )

    my_rows = pl.ds(pl.multiple_of(shard * ROWS, ROWS), ROWS)
    for k, u in enumerate((u0, u1)):

        def send(i, _):
            dy, dz = offsets(i)
            y_m, z_m = (y + dy) % 8, (z + dz) % 8
            x_m = x_of(y_m)
            m = z_m * 8 + y_m
            here = (dy == 0) & (dz == 0) & self_a

            @pl.when(jnp.logical_not(here))
            def _():
                pltpu.make_async_remote_copy(
                    u.at[m], own.at[k, my_rows], send_a.at[k], recv_a.at[k],
                    device_id=device(x_m, y_m, z_m, core), device_id_type=MESH,
                ).start()

            @pl.when(here)
            def _():
                pltpu.make_async_copy(u.at[m], own.at[k, my_rows], recv_a.at[k]).start()

            return 0

        lax.fori_loop(0, 64, send, 0)

    wait_bytes(own.at[0], recv_a.at[0])
    first[...] = newton_schulz(own[0])
    wait_bytes(own.at[1], recv_a.at[1])
    second = newton_schulz(own[1])
    total = (scale_step * first[...].astype(f32) + scale_step * second.astype(f32)).astype(bf16).T
    for zz in range(8):
        for yh in range(2):
            for xx in range(4):
                row = zz * 128 + yh * 64 + xx * 16
                delta[xx * 2 + zz // 4, pl.ds((zz % 4) * 32 + yh * 16, 16), :] = total[row : row + 16]

    me = x * 2 + core
    copies = []
    for j in range(1, 8):
        tx, tc = (x + j // 2) % 4, (core + j) % 2
        copy = pltpu.make_async_remote_copy(
            delta.at[tx * 2 + tc], parts.at[j], send_b.at[j], recv_b.at[j],
            device_id=device(tx, y, z, tc), device_id_type=MESH,
        )
        copy.start()
        copies.append(copy)
    summed = delta[me].astype(f32)
    for j, copy in enumerate(copies):
        copy.wait_recv()
        summed = summed + parts[j + 1].astype(f32)
    summed = summed.astype(bf16)
    for i in range(64):
        reduced[i] = summed[2 * i : 2 * i + 2]

    def scatter(i, _):
        yy, tz, tc = i % 8, (i // 8) % 4, i // 32
        ty = (y + yy) % 8
        tz_all = core * 4 + (z + tz) % 4
        tcore = (core + tc) % 2
        piece = (tz_all % 4) * 16 + (ty // 4) * 8 + (ty % 4) * 2 + tcore
        here = (ty == y) & (tz_all == z) & (tcore == core)

        @pl.when(jnp.logical_not(here))
        def _():
            pltpu.make_async_remote_copy(
                reduced.at[piece], gathered.at[mine], send_c, recv_c,
                device_id=device(x, ty, tz_all, tcore), device_id_type=MESH,
            ).start()

        @pl.when(here)
        def _():
            pltpu.make_async_copy(reduced.at[piece], gathered.at[mine], recv_c).start()

        return 0

    lax.fori_loop(0, 64, scatter, 0)
    wait_bytes(gathered, recv_c)
    out[...] = gathered[...]

    for k in range(2):

        @pl.when(self_a)
        def _():
            wait_bytes(own.at[k, pl.ds(0, 63 * ROWS)], send_a.at[k])

        @pl.when(jnp.logical_not(self_a))
        def _():
            wait_bytes(own.at[k], send_a.at[k])

    for copy in copies:
        copy.wait_send()

    @pl.when(self_c)
    def _():
        wait_bytes(reduced.at[pl.ds(0, 63)], send_c)

    @pl.when(jnp.logical_not(self_c))
    def _():
        wait_bytes(reduced, send_c)


def exchange(u0, u1):
    vmem = pl.BlockSpec(memory_space=pltpu.VMEM)
    dma = pltpu.SemaphoreType.DMA
    return pl.pallas_call(
        exchange_kernel,
        out_shape=jax.ShapeDtypeStruct((MATS, 2, FF), bf16),
        in_specs=[vmem, vmem],
        out_specs=vmem,
        scratch_shapes=[
            pltpu.VMEM((INNER, D, FF), bf16),
            pltpu.VMEM((FF, D), bf16),
            pltpu.VMEM((8, 128, FF), bf16),
            pltpu.VMEM((8, 128, FF), bf16),
            pltpu.VMEM((64, 2, FF), bf16),
            pltpu.VMEM((64, 2, FF), bf16),
            dma((INNER,)), dma((INNER,)), dma((8,)), dma((8,)), dma, dma,
        ],
        compiler_params=pltpu.CompilerParams(
            collective_id=0, has_side_effects=True, vmem_limit_bytes=40 << 20
        ),
        name="muon_exchange",
    )(u0, u1)


def body(gradients, momentum, params, outer_moment, shadow):
    replica_count = lax.axis_size("replica")
    moment_now = momentum[0]
    updates = []
    for position in range(INNER):
        grad_now = gradients[0, position].astype(f32)
        moment_now = inner_beta * moment_now + grad_now
        updates.append((grad_now + inner_beta * moment_now).astype(bf16))
    summed = exchange(*updates)
    outer_delta = summed.astype(f32) / replica_count
    new_outer = outer_mu * outer_moment + outer_delta
    new_params = params - outer_rate * (outer_delta + outer_mu * new_outer)
    new_shadow = shadow_decay * shadow + (1.0 - shadow_decay) * new_params
    return (new_params, new_outer, new_shadow, moment_now[None])


def solution(mesh):
    state = P(None, ("shard", "replica"), None)
    momentum = P("replica", None, "shard", None)
    return jax.shard_map(
        body,
        mesh=mesh,
        in_specs=(P("replica", None, None, "shard", None), momentum, state, state, state),
        out_specs=(state, state, state, momentum),
        check_vma=False,
    )
```

```python
import functools
import math

import jax
import jax.numpy as jnp
from jax import lax
from jax.experimental import pallas as pl
from jax.experimental.pallas import tpu as pltpu
from jax.sharding import PartitionSpec as P

D = 1024
FF = 256
INNER = 2
NS_ITERS = 5
MATS = 64
ROWS = 16
CHUNKS = 4
PER_CHUNK = MATS // CHUNKS

quintic_a = 3.4445
quintic_b = -4.775
quintic_c = 2.0315
inner_beta = 0.95
outer_mu = 0.9
outer_rate = 0.7
shadow_decay = 0.9
scale_step = 0.2 * math.sqrt(D)

MESH = pl.DeviceIdType.MESH
f32, bf16 = jnp.float32, jnp.bfloat16
NT = (((1,), (1,)), ((), ()))
NN = (((1,), (0,)), ((), ()))


def place():
    replica, shard = lax.axis_index("replica"), lax.axis_index("shard")
    core, y_lo = rem(replica, 2), div(replica, 2)
    x, y_hi, z = rem(shard, 4), rem(div(shard, 4), 2), div(shard, 8)
    return replica, shard, x, y_hi * 4 + y_lo, z, core


DZ_ORDER = (0, 2, 5, 1, 6, 4, 7, 3)
DY_ORDER = (0, 4, 5, 2, 6, 3, 7, 1)


def rem(a, b):
    return lax.rem(a, jnp.int32(b))


def div(a, b):
    return lax.div(a, jnp.int32(b))


def dot(a, b, dims):
    return lax.dot_general(a, b, dims, preferred_element_type=f32)


def normalized(update):
    wide = update.astype(f32)
    squares = jnp.sum(wide * wide)
    return (wide / (jnp.sqrt(squares) + 1e-07)).astype(bf16)


def polynomial(current):
    gram = dot(current, current, NT).astype(bf16)
    square = dot(gram, gram, NN)
    return (quintic_b * gram.astype(f32) + quintic_c * square).astype(bf16)


def advance(current, poly):
    return (quintic_a * current.astype(f32) + dot(poly, current, NN)).astype(bf16)


def until_last(update):
    current = normalized(update).T
    for _ in range(NS_ITERS - 1):
        current = advance(current, polynomial(current))
    return current, polynomial(current)


def wait_bytes(ref, sem):
    pltpu.make_async_copy(ref, ref, sem).wait()


def exchange_kernel(gradients, momentum, out, new_momentum, grad, moment, updates, own, first, last,
                    delta, swapped, half, parts, reduced, gathered,
                    load, send_a, recv_a, send_s, recv_s, send_b, recv_b, send_c, recv_c):
    replica, shard, x, y, z, core = place()
    mine = z * 8 + y
    y_lo, z_half = rem(y, 4), div(z, 4)
    x_of = lambda y_m: rem(y + y_m, 4)
    self_a = x_of(y) == x
    self_c = core == z_half

    loads = []
    for c in range(CHUNKS):
        part = pl.ds(c * PER_CHUNK, PER_CHUNK)
        loads.append([
            pltpu.make_async_copy(gradients.at[:, part], grad.at[:, part], load.at[c, 0]),
            pltpu.make_async_copy(momentum.at[part], moment.at[part], load.at[c, 1]),
        ])
    for pair in loads:
        for copy in pair:
            copy.start()

    barrier = pltpu.get_barrier_semaphore()

    def greet(replica, shard):
        pl.semaphore_signal(
            barrier, 1, device_id={"replica": replica, "shard": shard}, device_id_type=MESH
        )

    from_replica = rem(x + 8 - y, 4) * 2 + core

    def greet_a(i, _):
        greet(from_replica, rem(shard + i, 64))
        return 0

    lax.fori_loop(1, 64, greet_a, 0, unroll=9)

    @pl.when(jnp.logical_not(self_a))
    def _():
        greet(from_replica, shard)

    other = {"replica": y_lo * 2 + 1 - core, "shard": shard}
    ring = [{"replica": replica, "shard": shard - x + rem(x + j, 4)} for j in range(4)]
    for peer in (other, *ring[1:]):
        greet(**peer)

    for c, pair in enumerate(loads):
        for copy in pair:
            copy.wait()

        def step(i, _):
            m = c * PER_CHUNK + i
            now = moment[m]
            for k in range(INNER):
                wide = grad[k, m].astype(f32)
                now = inner_beta * now + wide
                updates[k, m] = (wide + inner_beta * now).astype(bf16)
            new_momentum[m] = now
            return 0

        lax.fori_loop(0, PER_CHUNK, step, 0, unroll=4)

    pl.semaphore_wait(barrier, 64 + 4 - self_a.astype(jnp.int32))

    my_rows = pl.ds(pl.multiple_of(shard * ROWS, ROWS), ROWS)
    layers = [rem(z + dz, 8) * 8 for dz in DZ_ORDER]
    for k in range(INNER):

        def send(a, _):
            for b in range(8):
                y_m = rem(y + (DY_ORDER[b] + a), 8)
                m = layers[b] + y_m

                def go():
                    pltpu.make_async_remote_copy(
                        updates.at[k, m], own.at[k, my_rows], send_a.at[k], recv_a.at[k],
                        device_id={
                            "replica": rem(y_m, 4) * 2 + core,
                            "shard": layers[b] + div(y_m, 4) * 4 + x_of(y_m),
                        },
                        device_id_type=MESH,
                    ).start()

                if b == 0:
                    pl.when((a > 0) | jnp.logical_not(self_a))(go)
                else:
                    go()
            return 0

        lax.fori_loop(0, 8, send, 0)

        @pl.when(self_a)
        def _():
            pltpu.make_async_copy(updates.at[k, mine], own.at[k, my_rows], recv_a.at[k]).start()

    wait_bytes(own.at[0], recv_a.at[0])
    first[...] = advance(*until_last(own[0]))
    wait_bytes(own.at[1], recv_a.at[1])
    last[...], poly = until_last(own[1])
    swaps = []
    for j in range(4):
        chunk = rem(2 * (1 - core) + j, 4)
        columns = pl.ds(pl.multiple_of(chunk * 256, 256), 256)
        second = advance(last[:, columns], poly)
        total = (scale_step * first[:, columns].astype(f32) + scale_step * second.astype(f32)).astype(bf16).T
        for zz in range(2):
            for yh in range(2):
                for xx in range(4):
                    row = zz * 128 + yh * 64 + xx * 16
                    to = (j % 2) * 64 + zz * 32 + yh * 16
                    delta[j // 2, xx, pl.ds(to, 16), :] = total[row : row + 16]
        if j < 2:
            rows = pl.ds(j * 64, 64)
            copy = pltpu.make_async_remote_copy(
                delta.at[0, :, rows], swapped.at[:, rows], send_s.at[j], recv_s.at[j],
                device_id=other, device_id_type=MESH,
            )
            copy.start()
            swaps.append(copy)

    for copy in swaps:
        copy.wait_recv()
    copies = {}
    for j in (2, 1, 3):
        to = rem(x + j, 4)
        half[j] = (delta[1, to].astype(f32) + swapped[to].astype(f32)).astype(bf16)
        copies[j] = pltpu.make_async_remote_copy(
            half.at[j], parts.at[j], send_b.at[j], recv_b.at[j],
            device_id=ring[j], device_id_type=MESH,
        )
        copies[j].start()
    summed = delta[1, x].astype(f32) + swapped[x].astype(f32)
    for j in (1, 3, 2):
        copies[j].wait_recv()
        summed = summed + parts[j].astype(f32)
    summed = summed.astype(bf16)
    for i in range(64):
        reduced[i] = summed[2 * i : 2 * i + 2]

    def scatter(q, _):
        ty = rem(y + 8 + div(8 - q, 2) * (rem(q, 2) * 2 - 1), 8)
        ty_lo, ty_hi = rem(ty, 4), div(ty, 4)
        for t in (2, 1, 3, 0):
            tz_lo = rem(z + t, 4)
            for tc in range(2):
                tcore = rem(core + tc, 2)
                piece = tz_lo * 16 + ty_hi * 8 + ty_lo * 2 + tcore

                def go():
                    pltpu.make_async_remote_copy(
                        reduced.at[piece], gathered.at[mine], send_c, recv_c,
                        device_id={
                            "replica": ty_lo * 2 + tcore,
                            "shard": core * 32 + tz_lo * 8 + ty_hi * 4 + x,
                        },
                        device_id_type=MESH,
                    ).start()

                if t == 0 and tc == 0:
                    pl.when((q < 7) | jnp.logical_not(self_c))(go)
                else:
                    go()
        return 0

    lax.fori_loop(0, 8, scatter, 0)

    @pl.when(self_c)
    def _():
        piece = rem(z, 4) * 16 + div(y, 4) * 8 + y_lo * 2 + core
        pltpu.make_async_copy(reduced.at[piece], gathered.at[mine], recv_c).start()

    wait_bytes(gathered, recv_c)
    out[...] = gathered[...]

    for k in range(2):

        @pl.when(self_a)
        def _():
            wait_bytes(own.at[k, pl.ds(0, 63 * ROWS)], send_a.at[k])

        @pl.when(jnp.logical_not(self_a))
        def _():
            wait_bytes(own.at[k], send_a.at[k])

    for copy in (*swaps, *copies.values()):
        copy.wait_send()

    @pl.when(self_c)
    def _():
        wait_bytes(reduced.at[pl.ds(0, 63)], send_c)

    @pl.when(jnp.logical_not(self_c))
    def _():
        wait_bytes(reduced, send_c)


def exchange(gradients, momentum):
    vmem = pl.BlockSpec(memory_space=pltpu.VMEM)
    anywhere = pl.BlockSpec(memory_space=pl.ANY)
    dma = pltpu.SemaphoreType.DMA
    return pl.pallas_call(
        exchange_kernel,
        out_shape=(
            jax.ShapeDtypeStruct((MATS, 2, FF), bf16),
            jax.ShapeDtypeStruct((MATS, ROWS, FF), f32),
        ),
        in_specs=[anywhere, anywhere],
        out_specs=(vmem, vmem),
        scratch_shapes=[
            pltpu.VMEM((INNER, MATS, ROWS, FF), bf16),
            pltpu.VMEM((MATS, ROWS, FF), f32),
            pltpu.VMEM((INNER, MATS, ROWS, FF), bf16),
            pltpu.VMEM((INNER, D, FF), bf16),
            pltpu.VMEM((FF, D), bf16),
            pltpu.VMEM((FF, D), bf16),
            pltpu.VMEM((2, 4, 128, FF), bf16),
            pltpu.VMEM((4, 128, FF), bf16),
            pltpu.VMEM((4, 128, FF), bf16),
            pltpu.VMEM((4, 128, FF), bf16),
            pltpu.VMEM((64, 2, FF), bf16),
            pltpu.VMEM((64, 2, FF), bf16),
            dma((CHUNKS, 2)), dma((INNER,)), dma((INNER,)), dma((2,)), dma((2,)), dma((4,)), dma((4,)), dma, dma,
        ],
        compiler_params=pltpu.CompilerParams(
            collective_id=0, has_side_effects=True, vmem_limit_bytes=52 << 20
        ),
        name="muon_exchange",
    )(gradients, momentum)


def outer_kernel(summed, moved, params, outer_moment, shadow, new_params, new_outer, new_shadow,
                 new_momentum, results, done, moved_done):
    keep = pltpu.make_async_copy(moved, new_momentum, moved_done)
    keep.start()
    copies = []
    for c in range(CHUNKS):
        part = pl.ds(c * PER_CHUNK, PER_CHUNK)
        outer_delta = summed[part].astype(f32) / 8
        outer = outer_mu * outer_moment[part] + outer_delta
        weights = params[part] - outer_rate * (outer_delta + outer_mu * outer)
        average = shadow_decay * shadow[part] + (1.0 - shadow_decay) * weights
        for i, (value, to) in enumerate(((weights, new_params), (outer, new_outer), (average, new_shadow))):
            results[i, part] = value
            copy = pltpu.make_async_copy(results.at[i, part], to.at[part], done.at[c, i])
            copy.start()
            copies.append(copy)
    for copy in copies:
        copy.wait()
    keep.wait()


def body(gradients, momentum, params, outer_moment, shadow):
    summed, moved = exchange(gradients[0], momentum[0])
    vmem = pl.BlockSpec(memory_space=pltpu.VMEM)
    anywhere = pl.BlockSpec(memory_space=pl.ANY)
    state = jax.ShapeDtypeStruct((MATS, 2, FF), f32)
    new_params, new_outer, new_shadow, new_momentum = pl.pallas_call(
        outer_kernel,
        out_shape=(state, state, state, jax.ShapeDtypeStruct((MATS, ROWS, FF), f32)),
        in_specs=[vmem] * 5,
        out_specs=(anywhere,) * 4,
        scratch_shapes=[
            pltpu.VMEM((3, MATS, 2, FF), f32),
            pltpu.SemaphoreType.DMA((CHUNKS, 3)),
            pltpu.SemaphoreType.DMA,
        ],
        compiler_params=pltpu.CompilerParams(vmem_limit_bytes=8 << 20),
        name="outer_step",
    )(summed, moved, params, outer_moment, shadow)
    return (new_params, new_outer, new_shadow, new_momentum[None])


def solution(mesh):
    state = P(None, ("shard", "replica"), None)
    momentum = P("replica", None, "shard", None)
    return jax.shard_map(
        body,
        mesh=mesh,
        in_specs=(P("replica", None, None, "shard", None), momentum, state, state, state),
        out_specs=(state, state, state, momentum),
        check_vma=False,
    )
```

```python
import functools
import math

import jax
import jax.numpy as jnp
from jax import lax
from jax.experimental import pallas as pl
from jax.experimental.pallas import tpu as pltpu
from jax.sharding import PartitionSpec as P

D = 1024
FF = 256
INNER = 2
NS_ITERS = 5
MATS = 64
ROWS = 16
CHUNKS = 4
PER_CHUNK = MATS // CHUNKS

quintic_a = 3.4445
quintic_b = -4.775
quintic_c = 2.0315
inner_beta = 0.95
outer_mu = 0.9
outer_rate = 0.7
shadow_decay = 0.9
scale_step = 0.2 * math.sqrt(D)

MESH = pl.DeviceIdType.MESH
f32, bf16 = jnp.float32, jnp.bfloat16
NT = (((1,), (1,)), ((), ()))
NN = (((1,), (0,)), ((), ()))


def place():
    replica, shard = lax.axis_index("replica"), lax.axis_index("shard")
    core, y_lo = rem(replica, 2), div(replica, 2)
    x, y_hi, z = rem(shard, 4), rem(div(shard, 4), 2), div(shard, 8)
    return replica, shard, x, y_hi * 4 + y_lo, z, core


DZ_ORDER = (0, 2, 5, 1, 6, 4, 7, 3)
DY_ORDER = (0, 4, 5, 2, 6, 3, 7, 1)
ORDER = [((DY_ORDER[b] + a) % 8, DZ_ORDER[b]) for a in range(8) for b in range(8)]
ORDER.sort(key=lambda o: min(o[0], 8 - o[0]) + min(o[1], 8 - o[1]) <= 2)


def rem(a, b):
    return lax.rem(a, jnp.int32(b))


def div(a, b):
    return lax.div(a, jnp.int32(b))


def dot(a, b, dims):
    return lax.dot_general(a, b, dims, preferred_element_type=f32)


def polynomial(gram):
    gram = gram.astype(bf16)
    square = dot(gram, gram, NN)
    return (quintic_b * gram.astype(f32) + quintic_c * square).astype(bf16)


def advance(current, poly):
    return (quintic_a * current.astype(f32) + dot(poly, current, NN)).astype(bf16)


def until_last(update):
    raw = update.T
    gram = dot(raw, raw, NT)
    row, column = (lax.broadcasted_iota(jnp.int32, gram.shape, i) for i in range(2))
    squares = jnp.sum(jnp.where(row == column, gram, 0.0))
    scale = 1.0 / (jnp.sqrt(squares) + 1e-07)
    poly = polynomial(gram * scale * scale)
    current = (raw.astype(f32) * scale).astype(bf16)
    for _ in range(NS_ITERS - 1):
        current = advance(current, poly)
        poly = polynomial(dot(current, current, NT))
    return current, poly


def wait_bytes(ref, sem):
    pltpu.make_async_copy(ref, ref, sem).wait()


def exchange_kernel(gradients, momentum, out, new_momentum, grad, moment, updates, own, first, last,
                    delta, swapped, half, parts, reduced, gathered,
                    load, send_a, recv_a, send_s, recv_s, send_b, recv_b, send_c, recv_c):
    replica, shard, x, y, z, core = place()
    mine = z * 8 + y
    y_lo, z_half = rem(y, 4), div(z, 4)
    x_of = lambda y_m: rem(y + y_m, 4)
    self_a = x_of(y) == x
    self_c = core == z_half

    loads = []
    for c in range(CHUNKS):
        part = pl.ds(c * PER_CHUNK, PER_CHUNK)
        loads.append([
            pltpu.make_async_copy(gradients.at[:, part], grad.at[:, part], load.at[c, 0]),
            pltpu.make_async_copy(momentum.at[part], moment.at[part], load.at[c, 1]),
        ])
    for pair in loads:
        for copy in pair:
            copy.start()

    barrier = pltpu.get_barrier_semaphore()

    def greet(replica, shard):
        pl.semaphore_signal(
            barrier, 1, device_id={"replica": replica, "shard": shard}, device_id_type=MESH
        )

    from_replica = rem(x + 8 - y, 4) * 2 + core

    def greet_a(i, _):
        greet(from_replica, rem(shard + i, 64))
        return 0

    lax.fori_loop(25, 64, greet_a, 0, unroll=13)
    lax.fori_loop(1, 25, greet_a, 0, unroll=12)

    @pl.when(jnp.logical_not(self_a))
    def _():
        greet(from_replica, shard)

    other = {"replica": y_lo * 2 + 1 - core, "shard": shard}
    ring = [{"replica": replica, "shard": shard - x + rem(x + j, 4)} for j in range(4)]
    for peer in (other, *ring[1:]):
        greet(**peer)

    for c, pair in enumerate(loads):
        for copy in pair:
            copy.wait()

        def step(i, _):
            m = c * PER_CHUNK + i
            now = moment[m]
            for k in range(INNER):
                wide = grad[k, m].astype(f32)
                now = inner_beta * now + wide
                updates[k, m] = (wide + inner_beta * now).astype(bf16)
            new_momentum[m] = now
            return 0

        lax.fori_loop(0, PER_CHUNK, step, 0, unroll=4)

    pl.semaphore_wait(barrier, 64 + 4 - self_a.astype(jnp.int32))

    my_rows = pl.ds(pl.multiple_of(shard * ROWS, ROWS), ROWS)
    across = []
    for dy in range(8):
        y_m = rem(y + dy, 8)
        across.append((y_m, rem(y_m, 4) * 2 + core, div(y_m, 4) * 4 + x_of(y_m)))
    layers = [rem(z + dz, 8) * 8 for dz in range(8)]

    def send(k, _):
        for dy, dz in ORDER:
            y_m, to_replica, to_column = across[dy]

            def go():
                pltpu.make_async_remote_copy(
                    updates.at[k, layers[dz] + y_m], own.at[k, my_rows], send_a.at[k], recv_a.at[k],
                    device_id={"replica": to_replica, "shard": layers[dz] + to_column},
                    device_id_type=MESH,
                ).start()

            if (dy, dz) == (0, 0):
                pl.when(jnp.logical_not(self_a))(go)
            else:
                go()

        @pl.when(self_a)
        def _():
            pltpu.make_async_copy(updates.at[k, mine], own.at[k, my_rows], recv_a.at[k]).start()

        return 0

    lax.fori_loop(0, INNER, send, 0)

    wait_bytes(own.at[0], recv_a.at[0])
    first[...] = advance(*until_last(own[0]))
    wait_bytes(own.at[1], recv_a.at[1])
    last[...], poly = until_last(own[1])
    swaps = []
    for j in range(4):
        chunk = rem(2 * (1 - core) + j, 4)
        columns = pl.ds(pl.multiple_of(chunk * 256, 256), 256)
        second = advance(last[:, columns], poly)
        total = (scale_step * first[:, columns].astype(f32) + scale_step * second.astype(f32)).astype(bf16).T
        for zz in range(2):
            for yh in range(2):
                for xx in range(4):
                    row = zz * 128 + yh * 64 + xx * 16
                    to = (j % 2) * 64 + zz * 32 + yh * 16
                    delta[j // 2, xx, pl.ds(to, 16), :] = total[row : row + 16]
        if j < 2:
            rows = pl.ds(j * 64, 64)
            copy = pltpu.make_async_remote_copy(
                delta.at[0, :, rows], swapped.at[:, rows], send_s.at[j], recv_s.at[j],
                device_id=other, device_id_type=MESH,
            )
            copy.start()
            swaps.append(copy)

    for copy in swaps:
        copy.wait_recv()
    copies = {}
    for j in (2, 1, 3):
        to = rem(x + j, 4)
        half[j] = (delta[1, to].astype(f32) + swapped[to].astype(f32)).astype(bf16)
        copies[j] = pltpu.make_async_remote_copy(
            half.at[j], parts.at[j], send_b.at[j], recv_b.at[j],
            device_id=ring[j], device_id_type=MESH,
        )
        copies[j].start()
    summed = delta[1, x].astype(f32) + swapped[x].astype(f32)
    for j in (1, 3, 2):
        copies[j].wait_recv()
        summed = summed + parts[j].astype(f32)
    summed = summed.astype(bf16)
    for i in range(64):
        reduced[i] = summed[2 * i : 2 * i + 2]

    def scatter(q, _):
        ty = rem(y + 8 + div(8 - q, 2) * (rem(q, 2) * 2 - 1), 8)
        ty_lo, ty_hi = rem(ty, 4), div(ty, 4)
        for t in (2, 1, 3, 0):
            tz_lo = rem(z + t, 4)
            for tc in range(2):
                tcore = rem(core + tc, 2)
                piece = tz_lo * 16 + ty_hi * 8 + ty_lo * 2 + tcore

                def go():
                    pltpu.make_async_remote_copy(
                        reduced.at[piece], gathered.at[mine], send_c, recv_c,
                        device_id={
                            "replica": ty_lo * 2 + tcore,
                            "shard": core * 32 + tz_lo * 8 + ty_hi * 4 + x,
                        },
                        device_id_type=MESH,
                    ).start()

                if t == 0 and tc == 0:
                    pl.when((q < 7) | jnp.logical_not(self_c))(go)
                else:
                    go()
        return 0

    lax.fori_loop(0, 8, scatter, 0)

    @pl.when(self_c)
    def _():
        piece = rem(z, 4) * 16 + div(y, 4) * 8 + y_lo * 2 + core
        pltpu.make_async_copy(reduced.at[piece], gathered.at[mine], recv_c).start()

    wait_bytes(gathered, recv_c)
    out[...] = gathered[...]

    for k in range(2):

        @pl.when(self_a)
        def _():
            wait_bytes(own.at[k, pl.ds(0, 63 * ROWS)], send_a.at[k])

        @pl.when(jnp.logical_not(self_a))
        def _():
            wait_bytes(own.at[k], send_a.at[k])

    for copy in (*swaps, *copies.values()):
        copy.wait_send()

    @pl.when(self_c)
    def _():
        wait_bytes(reduced.at[pl.ds(0, 63)], send_c)

    @pl.when(jnp.logical_not(self_c))
    def _():
        wait_bytes(reduced, send_c)


def exchange(gradients, momentum):
    vmem = pl.BlockSpec(memory_space=pltpu.VMEM)
    anywhere = pl.BlockSpec(memory_space=pl.ANY)
    dma = pltpu.SemaphoreType.DMA
    return pl.pallas_call(
        exchange_kernel,
        out_shape=(
            jax.ShapeDtypeStruct((MATS, 2, FF), bf16),
            jax.ShapeDtypeStruct((MATS, ROWS, FF), f32),
        ),
        in_specs=[anywhere, anywhere],
        out_specs=(vmem, vmem),
        scratch_shapes=[
            pltpu.VMEM((INNER, MATS, ROWS, FF), bf16),
            pltpu.VMEM((MATS, ROWS, FF), f32),
            pltpu.VMEM((INNER, MATS, ROWS, FF), bf16),
            pltpu.VMEM((INNER, D, FF), bf16),
            pltpu.VMEM((FF, D), bf16),
            pltpu.VMEM((FF, D), bf16),
            pltpu.VMEM((2, 4, 128, FF), bf16),
            pltpu.VMEM((4, 128, FF), bf16),
            pltpu.VMEM((4, 128, FF), bf16),
            pltpu.VMEM((4, 128, FF), bf16),
            pltpu.VMEM((64, 2, FF), bf16),
            pltpu.VMEM((64, 2, FF), bf16),
            dma((CHUNKS, 2)), dma((INNER,)), dma((INNER,)), dma((2,)), dma((2,)), dma((4,)), dma((4,)), dma, dma,
        ],
        compiler_params=pltpu.CompilerParams(
            collective_id=0, has_side_effects=True, vmem_limit_bytes=52 << 20
        ),
        name="muon_exchange",
    )(gradients, momentum)


def outer_kernel(summed, moved, params, outer_moment, shadow, new_params, new_outer, new_shadow,
                 new_momentum, results, done, moved_done):
    keep = pltpu.make_async_copy(moved, new_momentum, moved_done)
    keep.start()
    copies = []
    for c in range(CHUNKS):
        part = pl.ds(c * PER_CHUNK, PER_CHUNK)
        outer_delta = summed[part].astype(f32) / 8
        outer = outer_mu * outer_moment[part] + outer_delta
        weights = params[part] - outer_rate * (outer_delta + outer_mu * outer)
        average = shadow_decay * shadow[part] + (1.0 - shadow_decay) * weights
        for i, (value, to) in enumerate(((weights, new_params), (outer, new_outer), (average, new_shadow))):
            results[i, part] = value
            copy = pltpu.make_async_copy(results.at[i, part], to.at[part], done.at[c, i])
            copy.start()
            copies.append(copy)
    for copy in copies:
        copy.wait()
    keep.wait()


def body(gradients, momentum, params, outer_moment, shadow):
    summed, moved = exchange(gradients[0], momentum[0])
    vmem = pl.BlockSpec(memory_space=pltpu.VMEM)
    anywhere = pl.BlockSpec(memory_space=pl.ANY)
    state = jax.ShapeDtypeStruct((MATS, 2, FF), f32)
    new_params, new_outer, new_shadow, new_momentum = pl.pallas_call(
        outer_kernel,
        out_shape=(state, state, state, jax.ShapeDtypeStruct((MATS, ROWS, FF), f32)),
        in_specs=[vmem] * 5,
        out_specs=(anywhere,) * 4,
        scratch_shapes=[
            pltpu.VMEM((3, MATS, 2, FF), f32),
            pltpu.SemaphoreType.DMA((CHUNKS, 3)),
            pltpu.SemaphoreType.DMA,
        ],
        compiler_params=pltpu.CompilerParams(vmem_limit_bytes=8 << 20),
        name="outer_step",
    )(summed, moved, params, outer_moment, shadow)
    return (new_params, new_outer, new_shadow, new_momentum[None])


def solution(mesh):
    state = P(None, ("shard", "replica"), None)
    momentum = P("replica", None, "shard", None)
    return jax.shard_map(
        body,
        mesh=mesh,
        in_specs=(P("replica", None, None, "shard", None), momentum, state, state, state),
        out_specs=(state, state, state, momentum),
        check_vma=False,
    )
```
